32 devices in a mesh: hist: 8 (over z, x), cand: 4 (over y, core).
Axes of the slice: x: 2, y: 2, z: 4, core: 2. Of those that a mesh axis runs over, the one named last changes fastest.
Arguments:
- cand_emb: bfloat16 [4, 256, 1024], P('cand', 'hist'), may hold values from -6 to 6
- cand_user: int32 [4, 256], P('cand'), may hold values from 0 to 3
- kv_cache: bfloat16 [4, 64, 2, 128, 1024], P('cand', 'hist'), may hold values from -6 to 6
- tile_user: int32 [4, 64], P('cand', 'hist'), may hold values from 0 to 3
- tile_len: int32 [4, 64], P('cand', 'hist'), may hold values from 1 to 128
- w_uq: bfloat16 [2048, 1024], P('cand'), may hold values from -0.1875 to 0.1875
- w_out: bfloat16 [1024, 1024], P('cand'), may hold values from -0.1875 to 0.1875
Outputs:
- scored: bfloat16 [4, 256, 1024], P('cand', 'hist')
The draws below stay inside these ranges and needn't reach their ends.
All inputs are finite; a program needn't handle non-finite values.
Results may differ from the reference program's by a relative error of at most 0.0053.
Values may be sent and summed in bfloat16 or wider, within the bound.
A program may use at most 128 MiB of HBM per device.

```python
import math
import jax
import jax.numpy as jnp
import numpy as np
from jax import lax

D = 1024
HEADS = 8
TILE_ROWS = 128
TILE_DEV = 8
USERS_GRP = 4
GROUPS = 4
CANDS_GRP = 256
TILES_GRP = 64


def place_ends(values, stream_key, low, largest):
    longest = values.shape.index(max(values.shape))
    spots = []
    for shift in (0, 1):
        where = [jax.random.randint(jax.random.fold_in(stream_key, axis), (), 0, length) for axis, length in enumerate(values.shape)]
        where[longest] = (where[longest] + shift) % values.shape[longest]
        spots.append(tuple(where))
    return values.at[spots[0]].set(low).at[spots[1]].set(largest)


def block_levels(rng, shape, split, least, top_value):
    loudness = 1.0
    for position, blocks in split:
        heights = jax.random.uniform(jax.random.fold_in(jax.random.fold_in(rng, 6), position), (blocks,), jnp.float32, least / len(split), top_value / len(split))
        loudness = loudness * jnp.repeat(jnp.exp(heights), shape[position] // blocks).reshape((-1,) + (1,) * (len(shape) - 1 - position))
    return loudness


def rank_table(number_of, slope):
    portions = [(1 << 20) // math.isqrt(rank ** slope) + 1 for rank in range(1, number_of + 1)]
    scale = 1 + sum(portions) // (1 << 30)
    return np.cumsum(np.array([max(1, weight // scale) for weight in portions]))


def skewed_ids(own_key, shape, amount, lean):
    grid = rank_table(amount, lean)
    lot = jax.random.randint(jax.random.fold_in(own_key, 1), shape, 0, int(grid[amount - 1]))
    grade = jnp.searchsorted(jnp.asarray(grid, jnp.int32), lot, side="right")
    return jax.random.permutation(jax.random.fold_in(own_key, 2), amount)[grade].astype(jnp.int32)


def centred(key, dims, scale, bound, shards=(), held_as=jnp.bfloat16):
    array = scale * jax.random.normal(key, dims, jnp.float32)
    if shards:
        array = array * block_levels(key, dims, shards, -0.22, 0.18)
    return jnp.clip(array, -bound, bound).astype(held_as)


def setup_inputs(seed: int = 0) -> dict:
    seeds = jax.random.split(jax.random.key(seed), 8)
    return {
        "cand_emb": centred(seeds[0], (GROUPS, CANDS_GRP, D), 1.0, 6.0, ((0, 4), (1, 8))),
        "cand_user": place_ends(skewed_ids(seeds[1], (GROUPS, CANDS_GRP), USERS_GRP, 2), jax.random.fold_in(seeds[1], 3), 0, USERS_GRP - 1).astype(jnp.int32),
        "kv_cache": centred(seeds[2], (GROUPS, TILES_GRP, 2, TILE_ROWS, D), 1.0, 6.0, ((0, 4), (1, 8))),
        "tile_user": place_ends(jax.random.randint(seeds[3], (GROUPS, TILES_GRP), 0, USERS_GRP), jax.random.fold_in(seeds[3], 1), 0, USERS_GRP - 1).astype(jnp.int32),
        "tile_len": place_ends(jax.random.randint(seeds[4], (GROUPS, TILES_GRP), 1, TILE_ROWS + 1), jax.random.fold_in(seeds[4], 1), 1, TILE_ROWS).astype(jnp.int32),
        "w_uq": centred(seeds[5], (2 * D, D), D ** -0.5, 0.1875, ((0, 4),)),
        "w_out": centred(seeds[6], (D, D), D ** -0.5, 0.1875, ((0, 4),)),
    }


def reference(cand_emb, cand_user, kv_cache, tile_user, tile_len, w_uq, w_out):
    head_size = D // HEADS
    score_scale = 1.0 / head_size ** 0.5

    def one_group(inputs):
        embeds, users, caches, owners, lengths = inputs
        count = embeds.shape[0]
        uq_full = jnp.dot(embeds, w_uq.T, preferred_element_type=jnp.float32)
        uq_full = jax.nn.silu(uq_full).astype(jnp.bfloat16)
        u_part = uq_full[:, :D]
        queries = uq_full[:, D:].astype(jnp.float32).reshape(count, HEADS, head_size)
        blocks = caches.reshape(TILES_GRP // TILE_DEV, TILE_DEV, 2, TILE_ROWS, D)
        block_owner = owners.reshape(TILES_GRP // TILE_DEV, TILE_DEV)
        block_len = lengths.reshape(TILES_GRP // TILE_DEV, TILE_DEV)
        row_ids = jnp.arange(TILE_ROWS, dtype=jnp.int32)

        def step(total, item):
            block, who, lens = item
            keys = block[:, 0].astype(jnp.float32).reshape(TILE_DEV * TILE_ROWS, HEADS, head_size)
            values = block[:, 1].astype(jnp.float32).reshape(TILE_DEV * TILE_ROWS, HEADS, head_size)
            valid = (row_ids[None, :] < lens[:, None]).reshape(TILE_DEV * TILE_ROWS)
            whose = jnp.repeat(who, TILE_ROWS)
            allowed = (users[:, None] == whose[None, :]) & valid[None, :]
            scores = jnp.einsum('qhd,khd->hqk', queries, keys) * score_scale
            weights = jnp.where(allowed[None], jax.nn.silu(scores), 0.0).astype(jnp.bfloat16)
            weights = lax.optimization_barrier(weights).astype(jnp.float32)
            return (total + jnp.einsum('hqk,khd->qhd', weights, values), None)
        start_total = jnp.zeros((count, HEADS, head_size), jnp.float32)
        attn, _ = lax.scan(step, start_total, (blocks, block_owner, block_len))
        attn = attn.reshape(count, D)
        center = lax.optimization_barrier(jnp.mean(attn, axis=1, keepdims=True))
        spread = lax.optimization_barrier(jnp.mean((attn - center) ** 2, axis=1, keepdims=True))
        normed = (attn - center) / jnp.sqrt(spread + 1e-05)
        y_rows = (normed * u_part.astype(jnp.float32)).astype(jnp.bfloat16)
        projected = jnp.dot(y_rows, w_out.T, preferred_element_type=jnp.float32)
        return (embeds.astype(jnp.float32) + projected).astype(jnp.bfloat16)
    return lax.map(one_group, (cand_emb, cand_user, kv_cache, tile_user, tile_len))
```

```python
import functools

import jax
import jax.numpy as jnp
from jax import lax
from jax.experimental import pallas as pl
from jax.experimental.pallas import tpu as pltpu
from jax.sharding import PartitionSpec as P

HEADS = 8
BF16 = jnp.bfloat16
F32 = jnp.float32


def times_rows(left, slab):
    return lax.dot_general(left, slab, (((1,), (1,)), ((), ())), preferred_element_type=F32)


def half_silu(half):
    return half + half * jnp.tanh(half)


def loop(low, high, body):
    if high - low <= 8:
        for step in range(low, high):
            body(step)
    else:
        lax.fori_loop(low, high, lambda step, carry: (body(step), carry)[1], 0)


def kernel(
    nh, nc, emb_hbm, user_ref, kv_hbm, owner_ref, len_ref, wuq_hbm, wout_hbm, out_ref,
    emb, kv, wuq, wout, uq_send, uq_all, mask, part, landed,
    local_sem, emb_send, emb_recv, uq_ssem, uq_rsem, q_send, q_recv,
    part_send, part_recv, w_send, w_recv, wf_send, wf_recv,
):
    hist = lax.axis_index("hist")
    cand = lax.axis_index("cand")
    rows, width = emb.shape[1], emb.shape[2]
    feats = wuq.shape[0]
    slices = nc // 2
    head_size = width // HEADS
    tiles, tile_rows = kv.shape[0], kv.shape[2]
    chips = nc // 2
    mate = cand + 1 - 2 * lax.rem(cand, 2)

    def remote(src, dst, ssem, rsem, peer):
        return pltpu.make_async_remote_copy(
            src_ref=src, dst_ref=dst, send_sem=ssem, recv_sem=rsem,
            device_id=peer, device_id_type=pl.DeviceIdType.MESH,
        )

    def up_cand(step):
        return lax.rem(cand + step, nc)

    def down_cand(step):
        return lax.rem(cand + nc - step, nc)

    def up_hist(step):
        return lax.rem(hist + step, nh)

    def down_hist(step):
        return lax.rem(hist + nh - step, nh)

    load_emb = pltpu.make_async_copy(emb_hbm.at[0], emb.at[0], local_sem.at[0])
    load_wuq = pltpu.make_async_copy(wuq_hbm, wuq, local_sem.at[1])
    load_kv = pltpu.make_async_copy(kv_hbm.at[0], kv, local_sem.at[2])
    load_wout = pltpu.make_async_copy(wout_hbm, wout.at[cand], local_sem.at[3])
    load_emb.start()
    load_wuq.start()
    load_wout.start()
    load_kv.start()

    barrier = pltpu.get_barrier_semaphore()

    def greet_cand(step):
        pl.semaphore_signal(
            barrier, inc=1, device_id=(hist, up_cand(step)), device_id_type=pl.DeviceIdType.MESH
        )

    def greet_hist(step):
        pl.semaphore_signal(
            barrier, inc=1, device_id=(up_hist(step), cand), device_id_type=pl.DeviceIdType.MESH
        )

    loop(1, nc, greet_cand)
    loop(1, nh, greet_hist)
    pl.semaphore_wait(barrier, nc - 1 + nh - 1)

    def emb_copy(step):
        return remote(
            emb_hbm.at[0], emb.at[step], emb_send.at[step], emb_recv.at[step], (hist, up_cand(step))
        )

    loop(1, nc, lambda step: emb_copy(step).start())

    count = nh * rows
    users = jnp.broadcast_to(user_ref[...].astype(F32), (tile_rows, count)).T
    lane = lax.broadcasted_iota(jnp.int32, (count, tile_rows), 1)
    for tile in range(tiles):
        same = users == owner_ref[0, tile].astype(F32)
        valid = lane < len_ref[0, tile]
        mask[:, tile * tile_rows:(tile + 1) * tile_rows] = jnp.where(
            same & valid, 1.0, 0.0
        ).astype(BF16)

    load_wuq.wait()
    load_emb.wait()
    loop(1, nc, lambda step: emb_copy(step).wait())
    uq = times_rows(emb[...].reshape(nc * rows, width), wuq[...])
    uq = half_silu(uq * 0.5).astype(BF16).reshape(nc, rows, feats)
    uq_send[...] = uq
    uq_all[cand, hist] = uq[0]

    def uq_copy(step, slot):
        return remote(
            uq_send.at[step], uq_all.at[slot, hist], uq_ssem.at[step], uq_rsem.at[step],
            (hist, down_cand(step)),
        )

    loop(1, nc, lambda step: uq_copy(step, cand).start())

    def w_copy(step):
        return remote(
            wout_hbm, wout.at[cand], w_send.at[step], w_recv.at[step], (hist, up_cand(2 * step))
        )

    loop(1, chips, lambda step: w_copy(step).start())
    own_w = remote(wout_hbm, wout.at[cand], w_send.at[0], w_recv.at[0], (hist, mate))
    own_w.start()

    loop(1, nc, lambda step: uq_copy(step, up_cand(step)).wait())

    def q_copy(piece, step, slot):
        return remote(
            uq_all.at[slices + piece, slot], uq_all.at[slices + piece, slot],
            q_send.at[piece, step], q_recv.at[piece, step], (up_hist(step), cand),
        )

    for piece in range(slices):
        loop(1, nh, lambda step: q_copy(piece, step, hist).start())

    def part_copy(piece, step):
        peer = up_hist(step)
        return remote(
            part.at[piece, peer], landed.at[piece, step], part_send.at[piece, step],
            part_recv.at[piece, step], (peer, cand),
        )

    load_kv.wait()
    block = min(nh, 8)
    piece_heads = feats // head_size
    scale = 0.5 / head_size**0.5

    def attend(piece, head, base):
        cols = pl.ds(pl.multiple_of(head * head_size, head_size), head_size)
        here = pl.ds(pl.multiple_of((piece * piece_heads + head) * head_size, head_size), head_size)
        q = uq_all[slices + piece, pl.ds(base, block), :, cols].reshape(block * rows, head_size)
        k = kv[:, 0, :, here].reshape(tiles * tile_rows, head_size)
        v = kv[:, 1, :, here].reshape(tiles * tile_rows, head_size)
        weights = half_silu(times_rows(q, k) * scale).astype(BF16)
        weights = weights * mask[pl.ds(pl.multiple_of(base * rows, block * rows), block * rows), :]
        total = jnp.dot(weights, v, preferred_element_type=F32)
        part[piece, pl.ds(base, block), :, cols] = total.astype(BF16).reshape(block, rows, head_size)

    for piece in range(slices):
        loop(1, nh, lambda step: q_copy(piece, step, down_hist(step)).wait())

        def work(index, carry):
            attend(piece, lax.rem(index, piece_heads), (index // piece_heads) * block)
            return carry

        lax.fori_loop(0, piece_heads * (nh // block), work, 0)
        loop(1, nh, lambda step: part_copy(piece, step).start())

    def wf_copy(step):
        slot = down_cand(2 * step)
        return remote(wout.at[slot], wout.at[slot], wf_send.at[step], wf_recv.at[step], (hist, mate))

    def forward(step):
        w_copy(step).wait()
        wf_copy(step).start()

    loop(1, chips, forward)

    for piece in range(slices):
        loop(1, nh, lambda step: part_copy(piece, step).wait())
    attn = []
    for piece in range(slices):
        total = part[piece, hist].astype(F32)
        if nh <= 8:
            for step in range(1, nh):
                total = total + landed[piece, step].astype(F32)
        else:
            total = lax.fori_loop(
                1, nh, lambda step, acc: acc + landed[piece, step].astype(F32), total
            )
        attn.append(total)
    attn = jnp.concatenate(attn, axis=1)
    center = jnp.mean(attn, axis=1, keepdims=True)
    spread = jnp.mean((attn - center) ** 2, axis=1, keepdims=True)
    normed = (attn - center) / jnp.sqrt(spread + 1e-05)
    u = jnp.concatenate([uq_all[piece, hist] for piece in range(slices)], axis=1)
    y = (normed * u.astype(F32)).astype(BF16)

    own_w.wait()
    load_wout.wait()
    loop(1, chips, lambda step: wf_copy(step).wait())
    projected = times_rows(y, wout[...].reshape(width, width))
    out_ref[0] = (emb[0].astype(F32) + projected).astype(BF16)


def solution(mesh):
    nh, nc = mesh.shape["hist"], mesh.shape["cand"]

    def per_device(cand_emb, cand_user, kv_cache, tile_user, tile_len, w_uq, w_out):
        rows, width = cand_emb.shape[1:]
        tiles, _, tile_rows, _ = kv_cache.shape[1:]
        feats, outs = w_uq.shape[0], w_out.shape[0]
        slices = nc // 2
        dma = pltpu.SemaphoreType.DMA
        hbm = pl.BlockSpec(memory_space=pl.ANY)
        vmem = pl.BlockSpec(memory_space=pltpu.VMEM)
        smem = pl.BlockSpec(memory_space=pltpu.SMEM)
        return pl.pallas_call(
            functools.partial(kernel, nh, nc),
            out_shape=jax.ShapeDtypeStruct(cand_emb.shape, BF16),
            in_specs=[hbm, vmem, hbm, smem, smem, hbm, hbm],
            out_specs=vmem,
            scratch_shapes=[
                pltpu.VMEM((nc, rows, width), BF16),
                pltpu.VMEM((tiles, 2, tile_rows, width), BF16),
                pltpu.VMEM((feats, width), BF16),
                pltpu.VMEM((nc, outs, width), BF16),
                pltpu.VMEM((nc, rows, feats), BF16),
                pltpu.VMEM((nc, nh, rows, feats), BF16),
                pltpu.VMEM((nh * rows, tiles * tile_rows), BF16),
                pltpu.VMEM((slices, nh, rows, feats), BF16),
                pltpu.VMEM((slices, nh, rows, feats), BF16),
                dma((4,)),
                dma((nc,)), dma((nc,)),
                dma((nc,)), dma((nc,)),
                dma((slices, nh)), dma((slices, nh)),
                dma((slices, nh)), dma((slices, nh)),
                dma((nc // 2,)), dma((nc // 2,)),
                dma((nc // 2,)), dma((nc // 2,)),
            ],
            compiler_params=pltpu.CompilerParams(collective_id=0, has_side_effects=True),
        )(cand_emb, cand_user, kv_cache, tile_user, tile_len, w_uq, w_out)

    in_specs = (
        P("cand", "hist", None),
        P("cand", None),
        P("cand", "hist", None, None, None),
        P("cand", "hist"),
        P("cand", "hist"),
        P("cand", None),
        P("cand", None),
    )
    return jax.shard_map(
        per_device, mesh=mesh, in_specs=in_specs, out_specs=P("cand", "hist", None), check_vma=False
    )
```

```python
import functools

import jax
import jax.numpy as jnp
from jax import lax
from jax.experimental import pallas as pl
from jax.experimental.pallas import tpu as pltpu
from jax.sharding import PartitionSpec as P

HEADS = 8
BF16 = jnp.bfloat16
F32 = jnp.float32


def times_rows(left, slab):
    return lax.dot_general(left, slab, (((1,), (1,)), ((), ())), preferred_element_type=F32)


def half_silu(half):
    return half + half * jnp.tanh(half)


def loop(low, high, body):
    if high - low <= 8:
        for step in range(low, high):
            body(step)
    else:
        lax.fori_loop(low, high, lambda step, carry: (body(step), carry)[1], 0)


def kernel(
    nx, nz, nc, emb_hbm, user_ref, kv_hbm, owner_ref, len_ref, wuq_hbm, wout_hbm, out_ref,
    emb, kv, wuq, wout, uq_send, uq_all, mask, part, landed,
    local_sem, emb_send, emb_recv, uq_ssem, uq_rsem, q_send, q_recv,
    x_send, x_recv, part_send, part_recv, w_send, w_recv, wf_send, wf_recv, news,
):
    nh = nx * nz
    hist = lax.axis_index("hist")
    z, x = hist // nx, lax.rem(hist, nx)
    own_slot = x * nz + z
    cand = lax.axis_index("cand")
    rows, width = emb.shape[1], emb.shape[2]
    feats = wuq.shape[0]
    slices = nc // 2
    head_size = width // HEADS
    tiles, tile_rows = kv.shape[0], kv.shape[2]
    chips = nc // 2
    mate = cand + 1 - 2 * lax.rem(cand, 2)

    def remote(src, dst, ssem, rsem, peer):
        return pltpu.make_async_remote_copy(
            src_ref=src, dst_ref=dst, send_sem=ssem, recv_sem=rsem,
            device_id=peer, device_id_type=pl.DeviceIdType.MESH,
        )

    def up_cand(step):
        return lax.rem(cand + step, nc)

    def down_cand(step):
        return lax.rem(cand + nc - step, nc)

    def along_z(step):
        return lax.rem(z + nz + step, nz)

    def along_x(step):
        return lax.rem(x + nx + step, nx)

    def signal(sem, hist_to, cand_to):
        pl.semaphore_signal(
            sem, inc=1, device_id=(hist_to, cand_to), device_id_type=pl.DeviceIdType.MESH
        )

    load_emb = pltpu.make_async_copy(emb_hbm.at[0], emb.at[0], local_sem.at[0])
    load_wuq = pltpu.make_async_copy(wuq_hbm, wuq, local_sem.at[1])
    load_kv = pltpu.make_async_copy(kv_hbm.at[0], kv, local_sem.at[2])
    load_wout = pltpu.make_async_copy(wout_hbm, wout.at[cand], local_sem.at[3])
    load_emb.start()
    load_wuq.start()
    load_wout.start()
    load_kv.start()

    barrier = pltpu.get_barrier_semaphore()

    loop(1, nc, lambda step: signal(barrier, hist, up_cand(step)))
    loop(1, nx, lambda step: signal(barrier, z * nx + along_x(step), cand))
    low, high = z > 0, z < nz - 1
    pl.when(low)(lambda: signal(barrier, hist - nx, cand))
    pl.when(high)(lambda: signal(barrier, hist + nx, cand))
    pl.semaphore_wait(
        barrier, nc - 1 + nx - 1 + low.astype(jnp.int32) + high.astype(jnp.int32)
    )

    def emb_copy(step):
        return remote(
            emb_hbm.at[0], emb.at[step], emb_send.at[step], emb_recv.at[step], (hist, up_cand(step))
        )

    loop(1, nc, lambda step: emb_copy(step).start())

    for far in range(2, nz):
        pl.when((z >= far - 1) & (z < nz - 1))(lambda: signal(news.at[0], hist + nx, cand))
        pl.when((z + far - 1 < nz) & (z > 0))(lambda: signal(news.at[1], hist - nx, cand))
        pl.when(z >= far)(lambda: pl.semaphore_wait(news.at[0], 1))
        pl.when(z + far < nz)(lambda: pl.semaphore_wait(news.at[1], 1))

    count = nh * rows
    users = jnp.broadcast_to(user_ref[...].astype(F32), (tile_rows, count)).T
    lane = lax.broadcasted_iota(jnp.int32, (count, tile_rows), 1)
    for tile in range(tiles):
        same = users == owner_ref[0, tile].astype(F32)
        valid = lane < len_ref[0, tile]
        mask[:, :, :, tile * tile_rows:(tile + 1) * tile_rows] = jnp.where(
            same & valid, 1.0, 0.0
        ).astype(BF16).reshape(nz, nx, rows, tile_rows)

    load_wuq.wait()
    load_emb.wait()
    loop(1, nc, lambda step: emb_copy(step).wait())
    uq = times_rows(emb[...].reshape(nc * rows, width), wuq[...])
    uq = half_silu(uq * 0.5).astype(BF16).reshape(nc, rows, feats)
    uq_send[...] = uq
    uq_all[cand, own_slot] = uq[0]

    def uq_copy(step, slot):
        return remote(
            uq_send.at[step], uq_all.at[slot, own_slot], uq_ssem.at[step], uq_rsem.at[step],
            (hist, down_cand(step)),
        )

    loop(1, nc, lambda step: uq_copy(step, cand).start())

    def w_copy(step):
        return remote(
            wout_hbm, wout.at[cand], w_send.at[step], w_recv.at[step], (hist, up_cand(2 * step))
        )

    loop(1, chips, lambda step: w_copy(step).start())
    own_w = remote(wout_hbm, wout.at[cand], w_send.at[0], w_recv.at[0], (hist, mate))
    own_w.start()

    def await_slice(source):
        step = lax.rem(source + nc - cand, nc)
        pl.when(step > 0)(lambda: uq_copy(step, source).wait_recv())

    def zq_copy(piece, step, from_z):
        block = uq_all.at[slices + piece, x * nz + from_z]
        return remote(
            block, block, q_send.at[piece, step], q_recv.at[piece, step],
            (along_z(step) * nx + x, cand),
        )

    def xq_copy(piece, over, step, from_x):
        block = uq_all.at[slices + piece, from_x * nz + along_z(-step)]
        sem = over * nz + step
        return remote(
            block, block, x_send.at[piece, sem], x_recv.at[piece, sem],
            (z * nx + along_x(over), cand),
        )

    def part_copy(piece, over, step):
        to_z, to_x = along_z(step), along_x(over)
        place = over * nz + step
        return remote(
            part.at[piece, to_x * nz + to_z], landed.at[piece, place],
            part_send.at[piece, place], part_recv.at[piece, place], (to_z * nx + to_x, cand),
        )

    def spread(piece, step):
        loop(1, nx, lambda over: xq_copy(piece, over, step, x).start())

    for piece in range(slices):
        await_slice(slices + piece)
        loop(1, nz, lambda step: zq_copy(piece, step, z).start())
        spread(piece, 0)

    load_kv.wait()
    piece_heads = feats // head_size
    scale = 0.5 / head_size**0.5
    keys = tiles * tile_rows

    def attend(piece, column):
        base = column * nz

        def work(head, carry):
            cols = pl.ds(pl.multiple_of(head * head_size, head_size), head_size)
            first = (piece * piece_heads + head) * head_size
            here = pl.ds(pl.multiple_of(first, head_size), head_size)
            q = uq_all[slices + piece, pl.ds(base, nz), :, cols].reshape(nz * rows, head_size)
            k = kv[:, 0, :, here].reshape(keys, head_size)
            v = kv[:, 1, :, here].reshape(keys, head_size)
            weights = half_silu(times_rows(q, k) * scale).astype(BF16)
            weights = weights * mask[:, column].reshape(nz * rows, keys)
            total = jnp.dot(weights, v, preferred_element_type=F32)
            part[piece, pl.ds(base, nz), :, cols] = total.astype(BF16).reshape(nz, rows, head_size)
            return carry

        lax.fori_loop(0, piece_heads, work, 0)

    def arrive(piece, step):
        zq_copy(piece, step, along_z(-step)).wait_recv()
        spread(piece, step)

    for piece in range(slices):
        loop(1, nz, lambda step: arrive(piece, step))
        attend(piece, x)
        loop(1, nz, lambda step: part_copy(piece, 0, step).start())
    for piece in range(slices):
        for over in range(1, nx):
            loop(0, nz, lambda step: xq_copy(piece, over, step, along_x(-over)).wait_recv())
            attend(piece, along_x(-over))
            loop(0, nz, lambda step: part_copy(piece, nx - over, step).start())

    def wf_copy(step):
        slot = down_cand(2 * step)
        return remote(wout.at[slot], wout.at[slot], wf_send.at[step], wf_recv.at[step], (hist, mate))

    def forward(step):
        w_copy(step).wait()
        wf_copy(step).start()

    loop(1, chips, forward)

    for piece in range(slices):
        loop(1, nz, lambda step: zq_copy(piece, step, z).wait_send())
        loop(nz, nh, lambda at: xq_copy(piece, at // nz, lax.rem(at, nz), x).wait_send())
        loop(1, nh, lambda at: part_copy(piece, at // nz, lax.rem(at, nz)).wait())
    loop(1, nc, lambda step: uq_copy(step, cand).wait_send())
    loop(0, slices, await_slice)
    attn = []
    for piece in range(slices):
        total = part[piece, own_slot].astype(F32)
        if nh <= 8:
            for step in range(1, nh):
                total = total + landed[piece, step].astype(F32)
        else:
            total = lax.fori_loop(
                1, nh, lambda step, acc: acc + landed[piece, step].astype(F32), total
            )
        attn.append(total)
    attn = jnp.concatenate(attn, axis=1)
    center = jnp.mean(attn, axis=1, keepdims=True)
    spread = jnp.mean((attn - center) ** 2, axis=1, keepdims=True)
    normed = (attn - center) / jnp.sqrt(spread + 1e-05)
    u = jnp.concatenate([uq_all[piece, own_slot] for piece in range(slices)], axis=1)
    y = (normed * u.astype(F32)).astype(BF16)

    own_w.wait()
    load_wout.wait()
    loop(1, chips, lambda step: wf_copy(step).wait())
    projected = times_rows(y, wout[...].reshape(width, width))
    out_ref[0] = (emb[0].astype(F32) + projected).astype(BF16)


def solution(mesh):
    nh, nc = mesh.shape["hist"], mesh.shape["cand"]
    nx = 1 << ((nh.bit_length() - 1) // 2)
    nz = nh // nx

    def per_device(cand_emb, cand_user, kv_cache, tile_user, tile_len, w_uq, w_out):
        rows, width = cand_emb.shape[1:]
        tiles, _, tile_rows, _ = kv_cache.shape[1:]
        feats, outs = w_uq.shape[0], w_out.shape[0]
        slices = nc // 2
        dma = pltpu.SemaphoreType.DMA
        hbm = pl.BlockSpec(memory_space=pl.ANY)
        vmem = pl.BlockSpec(memory_space=pltpu.VMEM)
        smem = pl.BlockSpec(memory_space=pltpu.SMEM)
        return pl.pallas_call(
            functools.partial(kernel, nx, nz, nc),
            out_shape=jax.ShapeDtypeStruct(cand_emb.shape, BF16),
            in_specs=[hbm, vmem, hbm, smem, smem, hbm, hbm],
            out_specs=vmem,
            scratch_shapes=[
                pltpu.VMEM((nc, rows, width), BF16),
                pltpu.VMEM((tiles, 2, tile_rows, width), BF16),
                pltpu.VMEM((feats, width), BF16),
                pltpu.VMEM((nc, outs, width), BF16),
                pltpu.VMEM((nc, rows, feats), BF16),
                pltpu.VMEM((nc, nh, rows, feats), BF16),
                pltpu.VMEM((nz, nx, rows, tiles * tile_rows), BF16),
                pltpu.VMEM((slices, nh, rows, feats), BF16),
                pltpu.VMEM((slices, nh, rows, feats), BF16),
                dma((4,)),
                dma((nc,)), dma((nc,)),
                dma((nc,)), dma((nc,)),
                dma((slices, nz)), dma((slices, nz)),
                dma((slices, nh)), dma((slices, nh)),
                dma((slices, nh)), dma((slices, nh)),
                dma((nc // 2,)), dma((nc // 2,)),
                dma((nc // 2,)), dma((nc // 2,)),
                pltpu.SemaphoreType.REGULAR((2,)),
            ],
            compiler_params=pltpu.CompilerParams(collective_id=0, has_side_effects=True),
        )(cand_emb, cand_user, kv_cache, tile_user, tile_len, w_uq, w_out)

    in_specs = (
        P("cand", "hist", None),
        P("cand", None),
        P("cand", "hist", None, None, None),
        P("cand", "hist"),
        P("cand", "hist"),
        P("cand", None),
        P("cand", None),
    )
    return jax.shard_map(
        per_device, mesh=mesh, in_specs=in_specs, out_specs=P("cand", "hist", None), check_vma=False
    )
```

```python
import functools

import jax
import jax.numpy as jnp
from jax import lax
from jax.experimental import pallas as pl
from jax.experimental.pallas import tpu as pltpu
from jax.sharding import PartitionSpec as P

HEADS = 8
BF16 = jnp.bfloat16
F32 = jnp.float32


def times_rows(left, slab):
    return lax.dot_general(left, slab, (((1,), (1,)), ((), ())), preferred_element_type=F32)


def half_silu(half):
    return half + half * jnp.tanh(half)


def loop(low, high, body):
    if high - low <= 8:
        for step in range(low, high):
            body(step)
    else:
        lax.fori_loop(low, high, lambda step, carry: (body(step), carry)[1], 0)


def kernel(
    nx, nz, nc, emb_hbm, user_hbm, kv_hbm, owner_hbm, len_hbm, wuq_hbm, wout_hbm, out_ref,
    user_ref, owner_ref, len_ref, emb, kv, wuq, wout, uq_send, uq_all, mask, part, landed,
    local_sem, emb_send, emb_recv, uq_ssem, uq_rsem, q_send, q_recv,
    x_send, x_recv, part_send, part_recv, w_send, w_recv, wf_send, wf_recv, news, far_send,
):
    nh = nx * nz
    hist = lax.axis_index("hist")
    z, x = hist // nx, lax.rem(hist, nx)
    own_slot = x * nz + z
    cand = lax.axis_index("cand")
    rows, width = emb.shape[1], emb.shape[2]
    feats = wuq.shape[0]
    slices = nc // 2
    head_size = width // HEADS
    tiles, tile_rows = kv.shape[0], kv.shape[2]
    chips = nc // 2
    mate = cand + 1 - 2 * lax.rem(cand, 2)

    def remote(src, dst, ssem, rsem, peer):
        return pltpu.make_async_remote_copy(
            src_ref=src, dst_ref=dst, send_sem=ssem, recv_sem=rsem,
            device_id=peer, device_id_type=pl.DeviceIdType.MESH,
        )

    def up_cand(step):
        return lax.rem(cand + step, nc)

    def down_cand(step):
        return lax.rem(cand + nc - step, nc)

    def along_z(step):
        return lax.rem(z + nz + step, nz)

    def along_x(step):
        return lax.rem(x + nx + step, nx)

    def signal(sem, hist_to, cand_to):
        pl.semaphore_signal(
            sem, inc=1, device_id=(hist_to, cand_to), device_id_type=pl.DeviceIdType.MESH
        )

    load_emb = pltpu.make_async_copy(emb_hbm.at[0], emb.at[0], local_sem.at[0])
    load_wuq = pltpu.make_async_copy(wuq_hbm, wuq, local_sem.at[1])
    load_kv = pltpu.make_async_copy(kv_hbm.at[0], kv, local_sem.at[2])
    load_wout = pltpu.make_async_copy(wout_hbm, wout.at[cand], local_sem.at[3])
    load_small = [
        pltpu.make_async_copy(src, dst, local_sem.at[4 + at])
        for at, (src, dst) in enumerate(
            ((user_hbm, user_ref), (owner_hbm, owner_ref), (len_hbm, len_ref))
        )
    ]
    load_emb.start()
    for load in load_small:
        load.start()
    load_wuq.start()
    load_wout.start()
    load_kv.start()

    barrier = pltpu.get_barrier_semaphore()

    loop(1, nc, lambda step: signal(barrier, hist, up_cand(step)))
    loop(1, nx, lambda step: signal(barrier, z * nx + along_x(step), cand))
    low, high = z > 0, z < nz - 1
    pl.when(low)(lambda: signal(barrier, hist - nx, cand))
    pl.when(high)(lambda: signal(barrier, hist + nx, cand))
    pl.semaphore_wait(
        barrier, nc - 1 + nx - 1 + low.astype(jnp.int32) + high.astype(jnp.int32)
    )

    def emb_copy(step):
        return remote(
            emb_hbm.at[0], emb.at[step], emb_send.at[step], emb_recv.at[step], (hist, up_cand(step))
        )

    loop(1, nc, lambda step: emb_copy(step).start())

    for far in range(1, nz):
        pl.when((z >= far - 1) & (z < nz - 1))(lambda: signal(news.at[0], hist + nx, cand))
        pl.when((z + far - 1 < nz) & (z > 0))(lambda: signal(news.at[1], hist - nx, cand))
        pl.when(z >= far)(lambda: pl.semaphore_wait(news.at[0], 1))
        pl.when(z + far < nz)(lambda: pl.semaphore_wait(news.at[1], 1))

    for load in load_small:
        load.wait()
    count = nh * rows
    users = jnp.broadcast_to(user_ref[...].astype(F32), (tile_rows, count)).T
    lane = lax.broadcasted_iota(jnp.int32, (count, tile_rows), 1)
    for tile in range(tiles):
        same = users == owner_ref[0, tile].astype(F32)
        valid = lane < len_ref[0, tile]
        mask[:, :, :, tile * tile_rows:(tile + 1) * tile_rows] = jnp.where(
            same & valid, 1.0, 0.0
        ).astype(BF16).reshape(nz, nx, rows, tile_rows)

    load_wuq.wait()
    load_emb.wait()
    loop(1, nc, lambda step: emb_copy(step).wait())
    uq = times_rows(emb[...].reshape(nc * rows, width), wuq[...])
    uq = half_silu(uq * 0.5).astype(BF16).reshape(nc, rows, feats)
    uq_send[...] = uq
    uq_all[cand, own_slot] = uq[0]

    def uq_copy(step, slot):
        return remote(
            uq_send.at[step], uq_all.at[slot, own_slot], uq_ssem.at[step], uq_rsem.at[step],
            (hist, down_cand(step)),
        )

    loop(1, nc, lambda step: uq_copy(step, cand).start())

    half = nz // 2
    takes_far = cand < slices

    def far_copy(step):
        return remote(
            uq_send.at[step], uq_all.at[slices, own_slot], far_send.at[step], q_recv.at[0, half],
            (along_z(half) * nx + x, down_cand(step)),
        )

    def if_far(step, action):
        pl.when((cand == slices) & (down_cand(step) < slices))(lambda: action(far_copy(step)))

    loop(1, nc, lambda step: if_far(step, lambda copy: copy.start()))

    def w_copy(step):
        return remote(
            wout_hbm, wout.at[cand], w_send.at[step], w_recv.at[step], (hist, up_cand(2 * step))
        )

    loop(1, chips, lambda step: w_copy(step).start())
    own_w = remote(wout_hbm, wout.at[cand], w_send.at[0], w_recv.at[0], (hist, mate))
    own_w.start()

    def await_slice(source):
        step = lax.rem(source + nc - cand, nc)
        pl.when(step > 0)(lambda: uq_copy(step, source).wait_recv())

    def zq_copy(piece, step, from_z):
        block = uq_all.at[slices + piece, x * nz + from_z]
        return remote(
            block, block, q_send.at[piece, step], q_recv.at[piece, step],
            (along_z(step) * nx + x, cand),
        )

    def xq_copy(piece, over, step, from_x):
        block = uq_all.at[slices + piece, from_x * nz + along_z(-step)]
        sem = over * nz + step
        return remote(
            block, block, x_send.at[piece, sem], x_recv.at[piece, sem],
            (z * nx + along_x(over), cand),
        )

    def part_copy(piece, over, step):
        to_z, to_x = along_z(step), along_x(over)
        place = over * nz + step
        return remote(
            part.at[piece, to_x * nz + to_z], landed.at[piece, place],
            part_send.at[piece, place], part_recv.at[piece, place], (to_z * nx + to_x, cand),
        )

    def if_near(piece, step, action):
        if piece > 0:
            action(zq_copy(piece, step, z))
        else:
            pl.when(~takes_far | (step != half))(lambda: action(zq_copy(piece, step, z)))

    def spread(piece, step):
        loop(1, nx, lambda over: xq_copy(piece, over, step, x).start())

    for piece in range(slices):
        await_slice(slices + piece)
        loop(1, nz, lambda step: if_near(piece, step, lambda copy: copy.start()))
        spread(piece, 0)

    load_kv.wait()
    piece_heads = feats // head_size
    scale = 0.5 / head_size**0.5
    keys = tiles * tile_rows

    def attend(piece, column):
        base = column * nz

        def work(head, carry):
            cols = pl.ds(pl.multiple_of(head * head_size, head_size), head_size)
            first = (piece * piece_heads + head) * head_size
            here = pl.ds(pl.multiple_of(first, head_size), head_size)
            q = uq_all[slices + piece, pl.ds(base, nz), :, cols].reshape(nz * rows, head_size)
            k = kv[:, 0, :, here].reshape(keys, head_size)
            v = kv[:, 1, :, here].reshape(keys, head_size)
            weights = half_silu(times_rows(q, k) * scale).astype(BF16)
            weights = weights * mask[:, column].reshape(nz * rows, keys)
            total = jnp.dot(weights, v, preferred_element_type=F32)
            part[piece, pl.ds(base, nz), :, cols] = total.astype(BF16).reshape(nz, rows, head_size)
            return carry

        lax.fori_loop(0, piece_heads, work, 0)

    def arrive(piece, step):
        zq_copy(piece, step, along_z(-step)).wait_recv()
        spread(piece, step)

    for piece in range(slices):
        loop(1, nz, lambda step: arrive(piece, step))
        attend(piece, x)
        loop(1, nz, lambda step: part_copy(piece, 0, step).start())
    for piece in range(slices):
        for over in range(1, nx):
            loop(0, nz, lambda step: xq_copy(piece, over, step, along_x(-over)).wait_recv())
            attend(piece, along_x(-over))
            loop(0, nz, lambda step: part_copy(piece, nx - over, step).start())

    def wf_copy(step):
        slot = down_cand(2 * step)
        return remote(wout.at[slot], wout.at[slot], wf_send.at[step], wf_recv.at[step], (hist, mate))

    def forward(step):
        w_copy(step).wait()
        wf_copy(step).start()

    loop(1, chips, forward)

    for piece in range(slices):
        loop(1, nz, lambda step: if_near(piece, step, lambda copy: copy.wait_send()))
        loop(nz, nh, lambda at: xq_copy(piece, at // nz, lax.rem(at, nz), x).wait_send())
        loop(1, nh, lambda at: part_copy(piece, at // nz, lax.rem(at, nz)).wait())
    loop(1, nc, lambda step: uq_copy(step, cand).wait_send())
    loop(1, nc, lambda step: if_far(step, lambda copy: copy.wait_send()))
    loop(0, slices, await_slice)
    attn = []
    for piece in range(slices):
        total = part[piece, own_slot].astype(F32)
        if nh <= 8:
            for step in range(1, nh):
                total = total + landed[piece, step].astype(F32)
        else:
            total = lax.fori_loop(
                1, nh, lambda step, acc: acc + landed[piece, step].astype(F32), total
            )
        attn.append(total)
    attn = jnp.concatenate(attn, axis=1)
    center = jnp.mean(attn, axis=1, keepdims=True)
    spread = jnp.mean((attn - center) ** 2, axis=1, keepdims=True)
    normed = (attn - center) / jnp.sqrt(spread + 1e-05)
    u = jnp.concatenate([uq_all[piece, own_slot] for piece in range(slices)], axis=1)
    y = (normed * u.astype(F32)).astype(BF16)

    own_w.wait()
    load_wout.wait()
    loop(1, chips, lambda step: wf_copy(step).wait())
    projected = times_rows(y, wout[...].reshape(width, width))
    out_ref[0] = (emb[0].astype(F32) + projected).astype(BF16)


def solution(mesh):
    nh, nc = mesh.shape["hist"], mesh.shape["cand"]
    nx = 1 << ((nh.bit_length() - 1) // 2)
    nz = nh // nx

    def per_device(cand_emb, cand_user, kv_cache, tile_user, tile_len, w_uq, w_out):
        rows, width = cand_emb.shape[1:]
        tiles, _, tile_rows, _ = kv_cache.shape[1:]
        feats, outs = w_uq.shape[0], w_out.shape[0]
        slices = nc // 2
        dma = pltpu.SemaphoreType.DMA
        hbm = pl.BlockSpec(memory_space=pl.ANY)
        vmem = pl.BlockSpec(memory_space=pltpu.VMEM)
        return pl.pallas_call(
            functools.partial(kernel, nx, nz, nc),
            out_shape=jax.ShapeDtypeStruct(cand_emb.shape, BF16),
            in_specs=[hbm] * 7,
            out_specs=vmem,
            scratch_shapes=[
                pltpu.VMEM(cand_user.shape, jnp.int32),
                pltpu.SMEM(tile_user.shape, jnp.int32),
                pltpu.SMEM(tile_len.shape, jnp.int32),
                pltpu.VMEM((nc, rows, width), BF16),
                pltpu.VMEM((tiles, 2, tile_rows, width), BF16),
                pltpu.VMEM((feats, width), BF16),
                pltpu.VMEM((nc, outs, width), BF16),
                pltpu.VMEM((nc, rows, feats), BF16),
                pltpu.VMEM((nc, nh, rows, feats), BF16),
                pltpu.VMEM((nz, nx, rows, tiles * tile_rows), BF16),
                pltpu.VMEM((slices, nh, rows, feats), BF16),
                pltpu.VMEM((slices, nh, rows, feats), BF16),
                dma((7,)),
                dma((nc,)), dma((nc,)),
                dma((nc,)), dma((nc,)),
                dma((slices, nz)), dma((slices, nz)),
                dma((slices, nh)), dma((slices, nh)),
                dma((slices, nh)), dma((slices, nh)),
                dma((nc // 2,)), dma((nc // 2,)),
                dma((nc // 2,)), dma((nc // 2,)),
                pltpu.SemaphoreType.REGULAR((2,)),
                dma((nc,)),
            ],
            compiler_params=pltpu.CompilerParams(collective_id=0, has_side_effects=True),
        )(cand_emb, cand_user, kv_cache, tile_user, tile_len, w_uq, w_out)

    in_specs = (
        P("cand", "hist", None),
        P("cand", None),
        P("cand", "hist", None, None, None),
        P("cand", "hist"),
        P("cand", "hist"),
        P("cand", None),
        P("cand", None),
    )
    return jax.shard_map(
        per_device, mesh=mesh, in_specs=in_specs, out_specs=P("cand", "hist", None), check_vma=False
    )
```

```python
import functools

import jax
import jax.numpy as jnp
from jax import lax
from jax.experimental import pallas as pl
from jax.experimental.pallas import tpu as pltpu
from jax.sharding import PartitionSpec as P

HEADS = 8
BF16 = jnp.bfloat16
F32 = jnp.float32


def times_rows(left, slab):
    return lax.dot_general(left, slab, (((1,), (1,)), ((), ())), preferred_element_type=F32)


def half_silu(half):
    return half + half * jnp.tanh(half)


def loop(low, high, body):
    if high - low <= 8:
        for step in range(low, high):
            body(step)
    else:
        lax.fori_loop(low, high, lambda step, carry: (body(step), carry)[1], 0)


def kernel(
    nx, nz, nc, emb_hbm, user_hbm, kv_hbm, owner_hbm, len_hbm, wuq_hbm, wout_hbm, out_ref,
    user_ref, owner_ref, len_ref, emb, kv, wuq, wout, uq_send, uq_all, mask, part, landed,
    local_sem, emb_send, emb_recv, uq_ssem, uq_rsem, q_send, q_recv,
    x_send, x_recv, part_send, part_recv, w_send, w_recv, wf_send, wf_recv, news, far_send,
):
    nh = nx * nz
    hist = lax.axis_index("hist")
    z, x = hist // nx, lax.rem(hist, nx)
    own_slot = x * nz + z
    cand = lax.axis_index("cand")
    rows, width = emb.shape[1], emb.shape[2]
    feats = wuq.shape[0]
    slices = nc // 2
    head_size = width // HEADS
    tiles, tile_rows = kv.shape[0], kv.shape[2]
    chips = nc // 2
    mate = cand + 1 - 2 * lax.rem(cand, 2)

    def remote(src, dst, ssem, rsem, peer):
        return pltpu.make_async_remote_copy(
            src_ref=src, dst_ref=dst, send_sem=ssem, recv_sem=rsem,
            device_id=peer, device_id_type=pl.DeviceIdType.MESH,
        )

    def up_cand(step):
        return lax.rem(cand + step, nc)

    def down_cand(step):
        return lax.rem(cand + nc - step, nc)

    def along_z(step):
        return lax.rem(z + nz + step, nz)

    def along_x(step):
        return lax.rem(x + nx + step, nx)

    def signal(sem, hist_to, cand_to):
        pl.semaphore_signal(
            sem, inc=1, device_id=(hist_to, cand_to), device_id_type=pl.DeviceIdType.MESH
        )

    load_emb = pltpu.make_async_copy(emb_hbm.at[0], emb.at[0], local_sem.at[0])
    load_wuq = pltpu.make_async_copy(wuq_hbm, wuq, local_sem.at[1])
    load_kv = pltpu.make_async_copy(kv_hbm.at[0], kv, local_sem.at[2])
    load_wout = pltpu.make_async_copy(wout_hbm, wout.at[cand], local_sem.at[3])
    load_small = [
        pltpu.make_async_copy(src, dst, local_sem.at[4 + at])
        for at, (src, dst) in enumerate(
            ((user_hbm, user_ref), (owner_hbm, owner_ref), (len_hbm, len_ref))
        )
    ]
    load_emb.start()
    for load in load_small:
        load.start()
    load_wuq.start()
    load_wout.start()
    load_kv.start()

    barrier = pltpu.get_barrier_semaphore()

    loop(1, nc, lambda step: signal(barrier, hist, up_cand(step)))
    loop(1, nx, lambda step: signal(barrier, z * nx + along_x(step), cand))
    low, high = z > 0, z < nz - 1
    pl.when(low)(lambda: signal(barrier, hist - nx, cand))
    pl.when(high)(lambda: signal(barrier, hist + nx, cand))
    pl.semaphore_wait(
        barrier, nc - 1 + nx - 1 + low.astype(jnp.int32) + high.astype(jnp.int32)
    )

    def emb_copy(step):
        return remote(
            emb_hbm.at[0], emb.at[step], emb_send.at[step], emb_recv.at[step], (hist, up_cand(step))
        )

    loop(1, nc, lambda step: emb_copy(step).start())

    for far in range(1, nz):
        pl.when((z >= far - 1) & (z < nz - 1))(lambda: signal(news.at[0], hist + nx, cand))
        pl.when((z + far - 1 < nz) & (z > 0))(lambda: signal(news.at[1], hist - nx, cand))
        pl.when(z >= far)(lambda: pl.semaphore_wait(news.at[0], 1))
        pl.when(z + far < nz)(lambda: pl.semaphore_wait(news.at[1], 1))

    for load in load_small:
        load.wait()
    count = nh * rows
    users = jnp.broadcast_to(user_ref[...].astype(F32), (tile_rows, count)).T
    lane = lax.broadcasted_iota(jnp.int32, (count, tile_rows), 1)
    for tile in range(tiles):
        same = users == owner_ref[0, tile].astype(F32)
        valid = lane < len_ref[0, tile]
        mask[:, :, :, tile * tile_rows:(tile + 1) * tile_rows] = jnp.where(
            same & valid, 1.0, 0.0
        ).astype(BF16).reshape(nz, nx, rows, tile_rows)

    load_wuq.wait()
    load_emb.wait()
    loop(1, nc, lambda step: emb_copy(step).wait())
    uq = times_rows(emb[...].reshape(nc * rows, width), wuq[...])
    uq = half_silu(uq * 0.5).astype(BF16).reshape(nc, rows, feats)
    uq_send[...] = uq
    uq_all[cand, own_slot] = uq[0]

    def uq_copy(step, slot):
        return remote(
            uq_send.at[step], uq_all.at[slot, own_slot], uq_ssem.at[step], uq_rsem.at[step],
            (hist, down_cand(step)),
        )

    loop(1, nc, lambda step: uq_copy(step, cand).start())

    half = nz // 2
    takes_far = cand < slices

    def far_copy(step):
        return remote(
            uq_send.at[step], uq_all.at[slices, own_slot], far_send.at[step], q_recv.at[0, half],
            (along_z(half) * nx + x, down_cand(step)),
        )

    def if_far(step, action):
        pl.when((cand == slices) & (down_cand(step) < slices))(lambda: action(far_copy(step)))

    loop(1, nc, lambda step: if_far(step, lambda copy: copy.start()))

    def w_copy(step):
        return remote(
            wout_hbm, wout.at[cand], w_send.at[step], w_recv.at[step], (hist, up_cand(2 * step))
        )

    loop(1, chips, lambda step: w_copy(step).start())
    own_w = remote(wout_hbm, wout.at[cand], w_send.at[0], w_recv.at[0], (hist, mate))
    own_w.start()

    def await_slice(source):
        step = lax.rem(source + nc - cand, nc)
        pl.when(step > 0)(lambda: uq_copy(step, source).wait_recv())

    def zq_copy(piece, step, from_z):
        block = uq_all.at[slices + piece, x * nz + from_z]
        return remote(
            block, block, q_send.at[piece, step], q_recv.at[piece, step],
            (along_z(step) * nx + x, cand),
        )

    def xq_copy(piece, over, step, from_x):
        block = uq_all.at[slices + piece, from_x * nz + along_z(-step)]
        sem = over * nz + step
        return remote(
            block, block, x_send.at[piece, sem], x_recv.at[piece, sem],
            (z * nx + along_x(over), cand),
        )

    def part_copy(piece, over, step):
        to_z, to_x = along_z(step), along_x(over)
        place = over * nz + step
        return remote(
            part.at[piece, to_x * nz + to_z], landed.at[piece, place],
            part_send.at[piece, place], part_recv.at[piece, place], (to_z * nx + to_x, cand),
        )

    def if_near(piece, step, action):
        if piece > 0:
            action(zq_copy(piece, step, z))
        else:
            pl.when(~takes_far | (step != half))(lambda: action(zq_copy(piece, step, z)))

    def spread(piece, step):
        loop(1, nx, lambda over: xq_copy(piece, over, step, x).start())

    for piece in range(slices):
        await_slice(slices + piece)
        loop(1, nz, lambda step: if_near(piece, step, lambda copy: copy.start()))
        spread(piece, 0)

    load_kv.wait()
    piece_heads = feats // head_size
    scale = 0.5 / head_size**0.5
    keys = tiles * tile_rows

    def attend(piece, column):
        base = column * nz

        def work(head, carry):
            cols = pl.ds(pl.multiple_of(head * head_size, head_size), head_size)
            first = (piece * piece_heads + head) * head_size
            here = pl.ds(pl.multiple_of(first, head_size), head_size)
            q = uq_all[slices + piece, pl.ds(base, nz), :, cols].reshape(nz * rows, head_size)
            k = kv[:, 0, :, here].reshape(keys, head_size)
            v = kv[:, 1, :, here].reshape(keys, head_size)
            weights = half_silu(times_rows(q, k) * scale).astype(BF16)
            weights = weights * mask[:, column].reshape(nz * rows, keys)
            total = jnp.dot(weights, v, preferred_element_type=F32)
            part[piece, pl.ds(base, nz), :, cols] = total.astype(BF16).reshape(nz, rows, head_size)
            return carry

        lax.fori_loop(0, piece_heads, work, 0)

    def arrive(piece, step):
        zq_copy(piece, step, along_z(-step)).wait_recv()
        spread(piece, step)

    for piece in range(slices):
        loop(1, nz, lambda step: arrive(piece, step))
        attend(piece, x)
        loop(1, nz, lambda step: part_copy(piece, 0, step).start())
    for piece in range(slices):
        for over in range(1, nx):
            loop(0, nz, lambda step: xq_copy(piece, over, step, along_x(-over)).wait_recv())
            attend(piece, along_x(-over))
            loop(0, nz, lambda step: part_copy(piece, nx - over, step).start())

    def wf_copy(step):
        slot = down_cand(2 * step)
        return remote(wout.at[slot], wout.at[slot], wf_send.at[step], wf_recv.at[step], (hist, mate))

    def forward(step):
        w_copy(step).wait()
        wf_copy(step).start()

    loop(1, chips, forward)

    loop(0, slices, await_slice)
    attn = []
    for piece in range(slices):
        loop(1, nh, lambda at: part_copy(piece, at // nz, lax.rem(at, nz)).wait_recv())
        total = part[piece, own_slot].astype(F32)
        if nh <= 8:
            for step in range(1, nh):
                total = total + landed[piece, step].astype(F32)
        else:
            total = lax.fori_loop(
                1, nh, lambda step, acc: acc + landed[piece, step].astype(F32), total
            )
        attn.append(total)
    attn = jnp.concatenate(attn, axis=1)
    center = jnp.mean(attn, axis=1, keepdims=True)
    spread = jnp.mean((attn - center) ** 2, axis=1, keepdims=True)
    normed = (attn - center) / jnp.sqrt(spread + 1e-05)
    u = jnp.concatenate([uq_all[piece, own_slot] for piece in range(slices)], axis=1)
    y = (normed * u.astype(F32)).astype(BF16)

    own_w.wait()
    load_wout.wait()
    loop(1, chips, lambda step: wf_copy(step).wait())
    projected = times_rows(y, wout[...].reshape(width, width))
    out_ref[0] = (emb[0].astype(F32) + projected).astype(BF16)
    for piece in range(slices):
        loop(1, nz, lambda step: if_near(piece, step, lambda copy: copy.wait_send()))
        loop(nz, nh, lambda at: xq_copy(piece, at // nz, lax.rem(at, nz), x).wait_send())
        loop(1, nh, lambda at: part_copy(piece, at // nz, lax.rem(at, nz)).wait_send())
    loop(1, nc, lambda step: uq_copy(step, cand).wait_send())
    loop(1, nc, lambda step: if_far(step, lambda copy: copy.wait_send()))


def solution(mesh):
    nh, nc = mesh.shape["hist"], mesh.shape["cand"]
    nx = 1 << ((nh.bit_length() - 1) // 2)
    nz = nh // nx

    def per_device(cand_emb, cand_user, kv_cache, tile_user, tile_len, w_uq, w_out):
        rows, width = cand_emb.shape[1:]
        tiles, _, tile_rows, _ = kv_cache.shape[1:]
        feats, outs = w_uq.shape[0], w_out.shape[0]
        slices = nc // 2
        dma = pltpu.SemaphoreType.DMA
        hbm = pl.BlockSpec(memory_space=pl.ANY)
        vmem = pl.BlockSpec(memory_space=pltpu.VMEM)
        return pl.pallas_call(
            functools.partial(kernel, nx, nz, nc),
            out_shape=jax.ShapeDtypeStruct(cand_emb.shape, BF16),
            in_specs=[hbm] * 7,
            out_specs=vmem,
            scratch_shapes=[
                pltpu.VMEM(cand_user.shape, jnp.int32),
                pltpu.SMEM(tile_user.shape, jnp.int32),
                pltpu.SMEM(tile_len.shape, jnp.int32),
                pltpu.VMEM((nc, rows, width), BF16),
                pltpu.VMEM((tiles, 2, tile_rows, width), BF16),
                pltpu.VMEM((feats, width), BF16),
                pltpu.VMEM((nc, outs, width), BF16),
                pltpu.VMEM((nc, rows, feats), BF16),
                pltpu.VMEM((nc, nh, rows, feats), BF16),
                pltpu.VMEM((nz, nx, rows, tiles * tile_rows), BF16),
                pltpu.VMEM((slices, nh, rows, feats), BF16),
                pltpu.VMEM((slices, nh, rows, feats), BF16),
                dma((7,)),
                dma((nc,)), dma((nc,)),
                dma((nc,)), dma((nc,)),
                dma((slices, nz)), dma((slices, nz)),
                dma((slices, nh)), dma((slices, nh)),
                dma((slices, nh)), dma((slices, nh)),
                dma((nc // 2,)), dma((nc // 2,)),
                dma((nc // 2,)), dma((nc // 2,)),
                pltpu.SemaphoreType.REGULAR((2,)),
                dma((nc,)),
            ],
            compiler_params=pltpu.CompilerParams(collective_id=0, has_side_effects=True),
        )(cand_emb, cand_user, kv_cache, tile_user, tile_len, w_uq, w_out)

    in_specs = (
        P("cand", "hist", None),
        P("cand", None),
        P("cand", "hist", None, None, None),
        P("cand", "hist"),
        P("cand", "hist"),
        P("cand", None),
        P("cand", None),
    )
    return jax.shard_map(
        per_device, mesh=mesh, in_specs=in_specs, out_specs=P("cand", "hist", None), check_vma=False
    )
```
